512 devices in a mesh: dp: 32 (over x_lo, z, core), ctx: 16 (over y, x_hi).
Axes of the slice: x: 4 (x_hi: 2, x_lo: 2; x = x_hi * 2 + x_lo), y: 8, z: 8, core: 2. Of those that a mesh axis runs over, the one named last changes fastest.
Arguments:
- layer_input: bfloat16 [32, 2048, 8192], P('dp', 'ctx'), may hold values from -6 to 6
- queries: bfloat16 [32, 2048, 1024], P('dp', 'ctx'), may hold values from -68 to 68
- key_rows: bfloat16 [32, 2048, 128], P('dp', 'ctx'), may hold values from -4 to 4
- value_rows: bfloat16 [32, 2048, 128], P('dp', 'ctx'), may hold values from -5 to 5
- grad_output: bfloat16 [32, 2048, 1024], P('dp', 'ctx'), may hold values from -12 to 12
- segments: int32 [32, 2048], P('dp'), may hold values from 0 to 2, never falling along the last dimension, each value on 1 to 1024 neighbouring positions
- lengths: int32 [32], P('dp'), may hold values from 1024 to 2048, as said below
Outputs:
- grad_queries: bfloat16 [32, 2048, 1024], P('dp', 'ctx')
- grad_weights: bfloat16 [8192, 256], P(('dp', 'ctx'))
The draws below stay inside these ranges and needn't reach their ends.
Inputs may be any that keep to these rules, and one draw needn't show every extreme that they name: `lengths`: some rollout has all 2048 positions live.
All inputs are finite; a program needn't handle non-finite values.
Results may differ from the reference program's by a relative error of at most 0.0057.
Values may be sent and summed in bfloat16 or wider, within the bound.
No kernel may reach another device: no remote copies, remote signals or barrier semaphores. Data moves between devices by JAX's collectives and lax.ppermute only.
A program may use at most 64 MiB of HBM per device.

```python
import math
import jax
import jax.numpy as jnp
import numpy as np
from jax import lax

D = 8192
HD = 128
GROUP = 8
ROWS = 128
DOCS = 3
SPAN = 8
WINDOW = 1024
SEQ = 2048
ROLLOUTS = 32
N_DP = 32
N_CTX = 16


def shared_base(key):
    key_base = jnp.clip(jax.random.normal(jax.random.fold_in(key, 11), (ROLLOUTS, SEQ, HD), jnp.float32), -4.0, 4.0)
    return key_base


def draw_key_rows(key, part):
    key_base = shared_base(key)
    return key_base.astype(jnp.bfloat16)


def draw_queries(key, part):
    query_base = jnp.clip(jax.random.normal(jax.random.fold_in(key, 13), (ROLLOUTS, SEQ, GROUP * HD), jnp.float32), -4.0, 4.0)
    return query_base.astype(jnp.bfloat16)


def draw_lengths(key, part):
    picked = jax.random.randint(jax.random.fold_in(key, 21), (ROLLOUTS,), SEQ // 2, SEQ + 1)
    full_one = jax.random.randint(jax.random.fold_in(key, 22), (), 0, ROLLOUTS)
    return jnp.where(jnp.arange(ROLLOUTS) == full_one, SEQ, picked).astype(jnp.int32)


def strengthened(array, key, source, target, parts, factor):
    def block_of(position):
        return (jnp.arange(array.shape[position]) // (array.shape[position] // parts)).reshape((-1,) + (1,) * (array.ndim - 1 - position))

    one_side = jax.random.permutation(key, parts)[block_of(target)]
    far = (block_of(target) + parts // 2) % parts
    return jnp.where((block_of(source) == one_side) | (block_of(source) == far), factor * array, array)


def block_levels(stream_key, shape, cuts, low, high):
    level = 1.0
    for axis_at, shards_of in cuts:
        heights = jax.random.uniform(jax.random.fold_in(jax.random.fold_in(stream_key, 6), axis_at), (shards_of,), jnp.float32, low / len(cuts), high / len(cuts))
        level = level * jnp.repeat(jnp.exp(heights), shape[axis_at] // shards_of).reshape((-1,) + (1,) * (len(shape) - 1 - axis_at))
    return level


def length_profile(amount, total, most, lean):
    portions = [(1 << 20) // math.isqrt(standing ** lean) + 1 for standing in range(2, amount + 1)]
    rest, counts = total - most - (amount - 1), [1] * (amount - 1)
    while rest > 0:
        free = [i for i in range(amount - 1) if counts[i] < most]
        mass, budget = sum([portions[i] for i in free]), rest
        for i in free:
            extra = min(most - counts[i], max(1, budget * portions[i] // mass), rest)
            counts[i] = counts[i] + extra
            rest = rest - extra
    return np.array([most] + counts)


def uneven_parts(stream_key, amount, total, reach, skew):
    if amount == 2:
        one = jax.random.randint(stream_key, (), max(1, total - reach), min(reach, total - 1) + 1)
        return jnp.stack([one, total - one])
    sizes = jnp.asarray(length_profile(amount, total, reach, skew), jnp.int32)
    twos = (amount - 1) // 2
    giver, sink = sizes[1:1 + 2 * twos:2], sizes[2:2 + 2 * twos:2]
    margin = jnp.minimum(giver - 1, reach - sink)
    passed = jax.random.randint(jax.random.fold_in(stream_key, 1), (twos,), 0, 1 << 20) % (margin + 1)
    sizes = sizes.at[1:1 + 2 * twos:2].set(giver - passed).at[2:2 + 2 * twos:2].set(sink + passed)
    return sizes[jax.random.permutation(jax.random.fold_in(stream_key, 2), amount)]


def normal_values(key, shape, deviation, most, split=(), kind=jnp.bfloat16):
    entries = jax.random.normal(key, shape, jnp.float32) * deviation
    if len(split) > 0:
        entries = block_levels(key, shape, split, -0.22, 0.18) * entries
    return jnp.clip(entries, min=-most, max=most).astype(kind)


def heavy_noise(rng, shape, spread, reach, split, heavy, held_as=jnp.bfloat16):
    result = spread * jax.random.normal(rng, shape, jnp.float32)
    if split:
        result = result * block_levels(rng, shape, split, -0.22, 0.18)
    return jnp.clip(strengthened(result, jax.random.fold_in(rng, 3), *heavy), -reach, reach).astype(held_as)


def setup_inputs(seed: int = 0) -> dict:
    streams_of = jax.random.split(jax.random.key(seed), 8)
    layer_input = heavy_noise(streams_of[0], (ROLLOUTS, SEQ, D), 1.0, 6.0, ((0, 32), (1, 16)), (0, 2, 32, 2.75))
    queries = draw_queries(jax.random.fold_in(streams_of[7], 71), 0)
    key_rows = draw_key_rows(jax.random.fold_in(streams_of[7], 71), 0)
    value_rows = normal_values(streams_of[3], (ROLLOUTS, SEQ, HD), 1.0, 5.0, ((0, 32), (1, 16)))
    grad_output = normal_values(streams_of[4], (ROLLOUTS, SEQ, GROUP * HD), 2.0, 12.0, ((0, 32), (1, 16)))
    segments = jax.vmap(lambda own: jnp.searchsorted(jnp.cumsum(uneven_parts(own, DOCS, SEQ, SEQ // 2, 0)), jnp.arange(SEQ), side="right"))(jax.random.split(streams_of[5], ROLLOUTS)).reshape((ROLLOUTS, SEQ)).astype(jnp.int32)
    lengths = draw_lengths(jax.random.fold_in(streams_of[7], 71), 0)
    return dict(layer_input=layer_input, queries=queries, key_rows=key_rows, value_rows=value_rows, grad_output=grad_output, segments=segments, lengths=lengths)


def make_mask(query_seg, key_seg, query_pos, key_pos, length, window_len):
    gap = query_pos[:, None] - key_pos[None, :]
    same_doc = query_seg[:, None] == key_seg[None, :]
    inside = (gap >= 0) & (gap < window_len)
    alive = (key_pos[None, :] < length) | (gap == 0)
    return same_doc & inside & alive

def block_grads(query_blk, upstream, key_all, allowed, live, score_scale):
    head_size = key_all.shape[1] // 2
    key_part = key_all[:, :head_size].astype(jnp.float32)
    value_part = key_all[:, head_size:].astype(jnp.float32)
    query_f = query_blk.astype(jnp.float32)
    upstream_f = upstream.astype(jnp.float32)
    scores = jnp.einsum('rgd,kd->grk', query_f, key_part) * score_scale
    masked = jnp.where(allowed[None], scores, -1e+30)
    row_max = lax.optimization_barrier(jnp.max(masked, axis=2, keepdims=True))
    unnorm = jnp.where(allowed[None], jnp.exp(masked - row_max), 0.0)
    probs = unnorm / lax.optimization_barrier(jnp.sum(unnorm, axis=2, keepdims=True)) * live[None, :, None]
    probs_low = probs.astype(jnp.bfloat16).astype(jnp.float32)
    dprobs = jnp.einsum('rgd,kd->grk', upstream_f, value_part)
    row_dot = lax.optimization_barrier(jnp.sum(probs * dprobs, axis=2, keepdims=True))
    dscores = (probs * (dprobs - row_dot)).astype(jnp.bfloat16).astype(jnp.float32)
    grad_q = (jnp.einsum('grk,kd->rgd', dscores, key_part) * score_scale).astype(jnp.bfloat16)
    grad_k = jnp.einsum('grk,rgd->kd', dscores, query_f) * score_scale
    grad_v = jnp.einsum('grk,rgd->kd', probs_low, upstream_f)
    return (grad_q.reshape(query_blk.shape[0], -1), jnp.concatenate([grad_k, grad_v], axis=1))

def reference(layer_input, queries, key_rows, value_rows, grad_output, segments, lengths):
    window_len = WINDOW
    score_scale = 1.0 / math.sqrt(HD)

    def one_rollout(items):
        inputs_r, query_r, key_r, value_r, upstream_r, seg_r, length = items
        pair = jnp.concatenate([key_r, value_r], axis=1)
        pair_pad = jnp.concatenate([jnp.zeros((window_len, 2 * HD), jnp.bfloat16), pair], axis=0)
        seg_pad = jnp.concatenate([jnp.full((window_len,), -1, jnp.int32), seg_r.astype(jnp.int32)])

        def one_block(block):
            first_row = (block * ROWS).astype(jnp.int32)
            query_blk = lax.dynamic_slice_in_dim(query_r, first_row, ROWS, 0).reshape(ROWS, GROUP, HD)
            upstream = lax.dynamic_slice_in_dim(upstream_r, first_row, ROWS, 0).reshape(ROWS, GROUP, HD)
            key_all = lax.dynamic_slice_in_dim(pair_pad, first_row, window_len + ROWS, 0)
            query_seg = lax.dynamic_slice_in_dim(seg_r.astype(jnp.int32), first_row, ROWS, 0)
            key_seg = lax.dynamic_slice_in_dim(seg_pad, first_row, window_len + ROWS, 0)
            query_pos = first_row + jnp.arange(ROWS, dtype=jnp.int32)
            key_pos = first_row - window_len + jnp.arange(window_len + ROWS, dtype=jnp.int32)
            allowed = make_mask(query_seg, key_seg, query_pos, key_pos, length, window_len)
            live = (query_pos < length).astype(jnp.float32)
            return block_grads(query_blk, upstream, key_all, allowed, live, score_scale)
        grad_q, contrib = lax.map(one_block, jnp.arange(N_CTX, dtype=jnp.int32))
        contrib = contrib.reshape(N_CTX, SPAN + 1, ROWS, 2 * HD)
        total = jnp.zeros((N_CTX + SPAN, ROWS, 2 * HD), jnp.float32)
        for slot_index in range(SPAN + 1):
            total = total.at[slot_index:slot_index + N_CTX].add(contrib[:, slot_index])
        grad_kv = total[SPAN:].reshape(SEQ, 2 * HD).astype(jnp.bfloat16)
        rollout_grad = jnp.dot(inputs_r.T, grad_kv, preferred_element_type=jnp.float32)
        return (grad_q.reshape(SEQ, GROUP * HD), rollout_grad)
    grad_queries, rollout_grads = lax.map(one_rollout, (layer_input, queries, key_rows, value_rows, grad_output, segments, lengths))
    summed = lax.optimization_barrier(jnp.sum(rollout_grads, axis=0))
    grad_weights = (summed / N_DP).astype(jnp.bfloat16)
    return (grad_queries, grad_weights)
```

```python
import math

import jax
import jax.numpy as jnp
from jax import lax
from jax.sharding import Mesh, PartitionSpec as P


DP = ("x_lo", "z", "core")
CTX = ("y", "x_hi")


def make_mask(query_seg, key_seg, query_pos, key_pos, length, window_len):
    gap = query_pos[:, None] - key_pos[None, :]
    same_doc = query_seg[:, None] == key_seg[None, :]
    inside = (gap >= 0) & (gap < window_len)
    alive = (key_pos[None, :] < length) | (gap == 0)
    return same_doc & inside & alive


def block_grads(query_blk, upstream, key_all, allowed, live, score_scale):
    head_size = key_all.shape[1] // 2
    key_part = key_all[:, :head_size]
    value_part = key_all[:, head_size:]
    scores = (
        jnp.einsum("rgd,kd->grk", query_blk, key_part, preferred_element_type=jnp.float32)
        * score_scale
    )
    masked = jnp.where(allowed[None], scores, -1e30)
    row_max = jnp.max(masked, axis=2, keepdims=True)
    unnorm = jnp.where(allowed[None], jnp.exp(masked - row_max), 0.0)
    probs = unnorm / jnp.sum(unnorm, axis=2, keepdims=True) * live[None, :, None]
    probs_low = probs.astype(jnp.bfloat16)
    dprobs = jnp.einsum("rgd,kd->grk", upstream, value_part, preferred_element_type=jnp.float32)
    row_dot = jnp.sum(probs * dprobs, axis=2, keepdims=True)
    dscores = (probs * (dprobs - row_dot)).astype(jnp.bfloat16)
    grad_q = (
        jnp.einsum("grk,kd->rgd", dscores, key_part, preferred_element_type=jnp.float32)
        * score_scale
    ).astype(jnp.bfloat16)
    grad_k = (
        jnp.einsum("grk,rgd->kd", dscores, query_blk, preferred_element_type=jnp.float32)
        * score_scale
    )
    grad_v = jnp.einsum("grk,rgd->kd", probs_low, upstream, preferred_element_type=jnp.float32)
    return (grad_q.reshape(query_blk.shape[0], -1), jnp.concatenate([grad_k, grad_v], axis=1))


def y_shift(x, by):
    count = lax.axis_size("y")
    return lax.ppermute(x, "y", [(i, i + by) for i in range(count) if 0 <= i + by < count])


def flipped(x, axis):
    return lax.ppermute(x, axis, [(0, 1), (1, 0)])


def quad_swap(x, flip_x, flip_core):
    pairs = []
    for i in range(4):
        pairs.append((i, i ^ (2 * flip_x + flip_core)))
    return lax.ppermute(x, ("x_lo", "core"), pairs)


QUAD = ((0, 1), (1, 0), (1, 1))


def shards(layer_input, queries, key_rows, value_rows, grad_output, segments, lengths):
    y_count = lax.axis_size("y")
    z_count = lax.axis_size("z")
    dp_count = 4 * z_count
    x_lo = lax.axis_index("x_lo")
    core = lax.axis_index("core")
    y_at = lax.axis_index("y")
    x_hi = lax.axis_index("x_hi")
    row_count = layer_input.shape[1]
    width_all = layer_input.shape[2]
    head_size = key_rows.shape[2]
    group_size = queries.shape[2] // head_size
    window_len = 8 * row_count
    pair_rows = 2 * row_count
    back = 4
    score_scale = 1.0 / math.sqrt(head_size)

    local_pair = jnp.concatenate([key_rows[0], value_rows[0]], axis=1)
    other_pair = flipped(local_pair, "x_hi")
    first_half = jnp.where(x_hi == 0, local_pair, other_pair)
    second_half = jnp.where(x_hi == 0, other_pair, local_pair)
    both = jnp.concatenate([first_half, second_half], axis=0)
    earlier = [y_shift(both, k) for k in range(1, back + 1)]
    key_all = jnp.concatenate(earlier[::-1] + [both], axis=0)

    slab = width_all // (2 * z_count * 2)
    columns = layer_input[0].reshape(row_count, 2, z_count, 2, slab)

    def piece(flip_x, flip_core):
        part = lax.dynamic_slice(
            columns,
            (0, x_lo ^ flip_x, 0, core ^ flip_core, 0),
            (row_count, 1, z_count, 1, slab),
        )
        return part.reshape(row_count, z_count * slab)

    inputs = [piece(0, 0)] + [quad_swap(piece(*q), *q) for q in QUAD]

    length = lengths[0]
    seg_row = segments[0]
    reach = back * pair_rows
    seg_pad = jnp.concatenate([jnp.full((reach,), -1, jnp.int32), seg_row])
    base = y_at * pair_rows
    first_row = base + x_hi * row_count
    query_seg = lax.dynamic_slice_in_dim(seg_row, first_row, row_count, 0)
    key_seg = lax.dynamic_slice_in_dim(seg_pad, base, reach + pair_rows, 0)
    query_pos = first_row + jnp.arange(row_count, dtype=jnp.int32)
    key_pos = base - reach + jnp.arange(reach + pair_rows, dtype=jnp.int32)
    allowed = make_mask(query_seg, key_seg, query_pos, key_pos, length, window_len)
    live = (query_pos < length).astype(jnp.float32)
    query_blk = queries[0].reshape(row_count, group_size, head_size)
    upstream = grad_output[0].reshape(row_count, group_size, head_size)
    grad_q, contrib = block_grads(query_blk, upstream, key_all, allowed, live, score_scale)

    blocks = contrib.reshape(back + 1, pair_rows, 2 * head_size)
    low = blocks.astype(jnp.bfloat16)
    total = blocks[back]
    for k in range(1, back + 1):
        total = total + y_shift(low[back - k], -k).astype(jnp.float32)
    halves = total.reshape(2, row_count, 2 * head_size)
    mine = lax.dynamic_slice_in_dim(halves, x_hi, 1, 0)[0]
    theirs = lax.dynamic_slice_in_dim(halves, 1 - x_hi, 1, 0)[0]
    grad_kv = mine + flipped(theirs.astype(jnp.bfloat16), "x_hi").astype(jnp.float32)
    grad_kv = grad_kv.astype(jnp.bfloat16)

    grads = [grad_kv] + [quad_swap(grad_kv, *q) for q in QUAD]
    partial_value = jnp.einsum(
        "rd,rc->dc",
        jnp.concatenate(inputs, axis=0),
        jnp.concatenate(grads, axis=0),
        preferred_element_type=jnp.float32,
    ).astype(jnp.bfloat16)
    peers = z_count * y_count * 2
    pieces = partial_value.reshape(peers, slab * z_count // peers, 2 * head_size)
    moved = lax.all_to_all(pieces, ("z", "y", "x_hi"), split_axis=0, concat_axis=0, tiled=True)
    summed = jnp.sum(moved.astype(jnp.float32), axis=0)
    grad_weights = (summed / dp_count).astype(jnp.bfloat16)
    return (grad_q.reshape(1, row_count, group_size * head_size), grad_weights)


def solution(mesh):
    devices = mesh.devices
    dp_count, ctx_count = devices.shape
    fine = Mesh(
        devices.reshape(2, dp_count // 4, 2, ctx_count // 2, 2),
        ("x_lo", "z", "core", "y", "x_hi"),
    )
    return jax.shard_map(
        shards,
        mesh=fine,
        in_specs=(
            P(DP, CTX, None),
            P(DP, CTX, None),
            P(DP, CTX, None),
            P(DP, CTX, None),
            P(DP, CTX, None),
            P(DP, None),
            P(DP),
        ),
        out_specs=(P(DP, CTX, None), P(DP + CTX, None)),
        check_vma=False,
    )
```

```python
import math

import jax
import jax.numpy as jnp
from jax import lax
from jax.experimental import pallas as pl
from jax.experimental.pallas import tpu as pltpu
from jax.sharding import Mesh, PartitionSpec as P


NAMES = ("x_lo", "z_hi", "z_lo", "core", "y", "x_hi")
DP = NAMES[:4]
CTX = NAMES[4:]
BACK = 4
NEG = -1e30
BF16 = jnp.bfloat16
F32 = jnp.float32


def contract(a, b, dim_a, dim_b):
    return lax.dot_general(
        a, b, (((dim_a,), (dim_b,)), ((), ())), preferred_element_type=F32
    )


def attention_kernel(scale, group, at_ref, rows_ref, live_ref, q_ref, up_ref, *refs):
    pairs = [r[...] for r in refs[: BACK + 1]]
    gq_ref, own_ref = refs[BACK + 1], refs[BACK + 2]
    out_refs = refs[BACK + 3 : 2 * BACK + 3]
    ds_ref, p_ref, bias_ref = refs[2 * BACK + 3 :]
    hd = pairs[0].shape[1] // 2
    rows = q_ref.shape[0]
    keys = jnp.concatenate([p[:, :hd] for p in pairs], axis=0)
    values = jnp.concatenate([p[:, hd:] for p in pairs], axis=0)
    live = jnp.concatenate([live_ref[...]] * 2, axis=1)
    low, high, place = (rows_ref[n : n + 1, :] for n in range(3))
    size = pairs[0].shape[0]
    for k in range(BACK + 1):
        key_place = at_ref[0] - k * size + lax.broadcasted_iota(jnp.int32, (size, rows), 0)
        allowed = ((key_place >= low) & (key_place < high)) | (key_place == place)
        bias_ref[k * size : (k + 1) * size, :] = jnp.where(allowed, 0.0, NEG)
    for h in range(0, group, 2):
        heads = [slice(g * hd, (g + 1) * hd) for g in (h, h + 1)]
        cols = slice(h * rows, (h + 2) * rows)
        q_two = jnp.concatenate([q_ref[:, s] for s in heads], axis=0)
        up_two = jnp.concatenate([up_ref[:, s] for s in heads], axis=0)
        bias = jnp.concatenate([bias_ref[...]] * 2, axis=1)
        scores = contract(keys, q_two, 1, 1) * scale + bias
        top = jnp.max(scores, axis=0, keepdims=True)
        raised = jnp.exp(scores - top)
        probs = raised * (live / jnp.sum(raised, axis=0, keepdims=True))
        dprobs = contract(values, up_two, 1, 1)
        rowdot = jnp.sum(probs * dprobs, axis=0, keepdims=True)
        dscores = (probs * (dprobs - rowdot)).astype(BF16)
        ds_ref[:, cols] = dscores
        p_ref[:, cols] = probs.astype(BF16)
        grad_q = (contract(dscores, keys, 0, 0) * scale).astype(BF16)
        for n, s in enumerate(heads):
            gq_ref[:, s] = grad_q[n * rows : (n + 1) * rows]
    q_all = jnp.concatenate([q_ref[:, g * hd : (g + 1) * hd] for g in range(group)], axis=0)
    up_all = jnp.concatenate([up_ref[:, g * hd : (g + 1) * hd] for g in range(group)], axis=0)
    grad_k = contract(ds_ref[...], q_all, 1, 0) * scale
    grad_v = contract(p_ref[...], up_all, 1, 0)
    own_ref[:, :hd] = grad_k[:size]
    own_ref[:, hd:] = grad_v[:size]
    for k, ref in enumerate(out_refs, 1):
        ref[:, :hd] = grad_k[k * size : (k + 1) * size].astype(BF16)
        ref[:, hd:] = grad_v[k * size : (k + 1) * size].astype(BF16)


def attention(base, bounds, live, queries, upstream, pairs, scale):
    rows, wide = queries.shape
    size, two = pairs[0].shape
    group = wide // (two // 2)
    total = size * (BACK + 1)

    def kernel(*refs):
        attention_kernel(scale, group, *refs)

    return pl.pallas_call(
        kernel,
        out_shape=[jax.ShapeDtypeStruct((rows, wide), BF16)]
        + [jax.ShapeDtypeStruct((size, two), F32)]
        + [jax.ShapeDtypeStruct((size, two), BF16)] * BACK,
        in_specs=[pl.BlockSpec(memory_space=pltpu.SMEM)]
        + [pl.BlockSpec(memory_space=pltpu.VMEM)] * (5 + BACK),
        scratch_shapes=[pltpu.VMEM((total, rows * group), BF16)] * 2
        + [pltpu.VMEM((total, rows), F32)],
        cost_estimate=pl.CostEstimate(
            flops=5 * 2 * total * rows * wide,
            bytes_accessed=4 * total * two,
            transcendentals=total * rows * group,
        ),
        compiler_params=pltpu.CompilerParams(vmem_limit_bytes=32 << 20),
        name="window_attention",
    )(base, bounds, live, queries, upstream, *pairs)


def weights_kernel(at_ref, *refs):
    inputs, grads, out_ref = refs[:4], refs[4:7], refs[7]
    rows = grads[0].shape[0] // 2
    total = None
    for n, x in enumerate(inputs):
        at = pl.ds(pl.multiple_of(at_ref[n % 2] * rows, rows), rows)
        if n < 2:
            parts = [grads[0][at, :], grads[1][at, :]]
        else:
            parts = [grads[2][0, at, :], grads[2][1, at, :]]
        term = contract(x[...], jnp.concatenate(parts, axis=0), 1, 0)
        total = term if total is None else total + term
    out_ref[...] = total.astype(BF16)


def weight_partials(at, inputs, grads, steps):
    count, deep = inputs[0].shape
    tall = count // steps
    wide = grads[0].shape[1]
    return pl.pallas_call(
        weights_kernel,
        out_shape=jax.ShapeDtypeStruct((count, wide), BF16),
        grid=(steps,),
        in_specs=[pl.BlockSpec(memory_space=pltpu.SMEM)]
        + [pl.BlockSpec((tall, deep), lambda j: (j, 0))] * 4
        + [pl.BlockSpec(grads[0].shape, lambda j: (0, 0))] * 2
        + [pl.BlockSpec(grads[2].shape, lambda j: (0, 0, 0))],
        out_specs=pl.BlockSpec((tall, wide), lambda j: (j, 0)),
        cost_estimate=pl.CostEstimate(
            flops=2 * count * wide * deep * 4,
            bytes_accessed=2 * deep * 4 * (count + wide),
            transcendentals=0,
        ),
        compiler_params=pltpu.CompilerParams(vmem_limit_bytes=16 << 20),
        name="weight_partials",
    )(at, *inputs, *grads)


def y_shift(x, by):
    count = lax.axis_size("y")
    return lax.ppermute(x, "y", [(i, i + by) for i in range(count) if 0 <= i + by < count])


def flipped(x, axis):
    return lax.ppermute(x, axis, [(0, 1), (1, 0)])


def z_x_swap(x, flip_z, flip_x):
    pairs = [(i, i ^ (2 * flip_z + flip_x)) for i in range(4)]
    return lax.ppermute(x, ("z_lo", "x_hi"), pairs)


STEPS = range(1, BACK + 1)


def step(layer_input, queries, key_rows, value_rows, grad_output, segments, lengths):
    y_count = lax.axis_size("y")
    z_high = lax.axis_size("z_hi")
    dp_count = 8 * z_high
    z_lo = lax.axis_index("z_lo")
    core = lax.axis_index("core")
    y_at = lax.axis_index("y")
    x_hi = lax.axis_index("x_hi")
    rows = layer_input.shape[1]
    width_all = layer_input.shape[2]
    head_size = key_rows.shape[2]
    window_len = 8 * rows
    pair_rows = 2 * rows
    scale = 1.0 / math.sqrt(head_size)

    local_pair = jnp.concatenate([key_rows[0], value_rows[0]], axis=1)
    other_pair = flipped(local_pair, "x_hi")
    both = jnp.concatenate(
        [
            jnp.where(x_hi == 0, local_pair, other_pair),
            jnp.where(x_hi == 0, other_pair, local_pair),
        ],
        axis=0,
    )
    pairs = [both]
    for k in range(1, BACK):
        pairs.append(y_shift(both, k))
    half = BACK // 2
    if y_count == 2 * BACK:
        first = [(i, (i - half) % y_count) for i in range(BACK)]
        second = [((i - half) % y_count, i + BACK) for i in range(BACK)]
        passing = lax.ppermute(both, "y", first)
        pairs.append(lax.ppermute(passing, "y", second))
    else:
        pairs.append(y_shift(both, BACK))

    steps = 2 * z_high
    fine = width_all // (steps * 2 * 2 * y_count * 2)
    count = steps * y_count * fine
    turned = layer_input[0].T
    columns = turned.reshape(steps, 2, 2, y_count, 2, fine, rows)
    to_core = lax.dynamic_slice(
        columns, (0, 0, 1 - core, 0, 0, 0, 0), (steps, 2, 1, y_count, 2, fine, rows)
    )
    from_core = flipped(to_core.reshape(4 * count, rows), "core")
    core_columns = from_core.reshape(steps, 2, y_count, 2, fine, rows)

    def piece(flip_z, flip_x):
        z_to, x_to = z_lo ^ flip_z, x_hi ^ flip_x
        mine = lax.dynamic_slice(
            columns, (0, z_to, core, 0, x_to, 0, 0), (steps, 1, 1, y_count, 1, fine, rows)
        )
        theirs = lax.dynamic_slice(
            core_columns, (0, z_to, 0, x_to, 0, 0), (steps, 1, y_count, 1, fine, rows)
        )
        return jnp.concatenate([mine.reshape(count, rows), theirs.reshape(count, rows)], axis=1)

    inputs = [piece(0, 0)]
    for flips in ((0, 1), (1, 0), (1, 1)):
        inputs.append(z_x_swap(piece(*flips), *flips))

    length = lengths[0]
    seg_row = segments[0]
    base = y_at * pair_rows
    first_row = base + x_hi * rows
    query_seg = lax.dynamic_slice_in_dim(seg_row, first_row, rows, 0)
    query_pos = first_row + jnp.arange(rows, dtype=jnp.int32)
    starts = [jnp.sum((seg_row < n).astype(jnp.int32)) for n in (1, 2)]
    start = jnp.where(query_seg == 0, 0, jnp.where(query_seg == 1, starts[0], starts[1]))
    bounds = jnp.stack(
        [jnp.maximum(start, query_pos - (window_len - 1)), jnp.minimum(query_pos, length), query_pos]
    )
    live = (query_pos < length).astype(F32)[None, :]

    grad_q, own, *low = attention(
        base[None], bounds, live, queries[0], grad_output[0], pairs, scale
    )

    total = own
    for k in STEPS:
        came = y_shift(low[k - 1], -k)
        total = total + came.astype(F32)
    came = flipped(total.astype(BF16), "x_hi")
    grad_kv = (total + came.astype(F32)).astype(BF16)
    core_grad = flipped(grad_kv, "core")
    z_grads = flipped(jnp.stack([grad_kv, core_grad]), "z_lo")
    at = jnp.stack([x_hi, 1 - x_hi]).astype(jnp.int32)
    partial_value = weight_partials(at, inputs, [grad_kv, core_grad, z_grads], BACK)

    peers = steps * y_count
    pieces = partial_value.reshape(peers, fine, 2 * head_size)
    moved = lax.all_to_all(pieces, ("x_lo", "z_hi", "y"), split_axis=0, concat_axis=0, tiled=True)
    summed = jnp.sum(moved.astype(F32), axis=0)
    grad_weights = (summed / dp_count).astype(BF16)
    return (grad_q[None], grad_weights)


def solution(mesh):
    devices = mesh.devices
    dp_count, ctx_count = devices.shape
    fine = Mesh(devices.reshape(2, dp_count // 8, 2, 2, ctx_count // 2, 2), NAMES)
    return jax.shard_map(
        step,
        mesh=fine,
        in_specs=(
            P(DP, CTX, None),
            P(DP, CTX, None),
            P(DP, CTX, None),
            P(DP, CTX, None),
            P(DP, CTX, None),
            P(DP, None),
            P(DP),
        ),
        out_specs=(P(DP, CTX, None), P(NAMES, None)),
        check_vma=False,
    )
```

```python
import math

import jax
import jax.numpy as jnp
from jax import lax
from jax.experimental import pallas as pl
from jax.experimental.pallas import tpu as pltpu
from jax.sharding import Mesh, PartitionSpec as P


NAMES = ("x_lo", "z", "core", "y", "x_hi")
DP = NAMES[:3]
CTX = NAMES[3:]
BACK = 4
NEG = -1e30
BF16 = jnp.bfloat16
F32 = jnp.float32


def contract(a, b, dim_a, dim_b):
    return lax.dot_general(
        a, b, (((dim_a,), (dim_b,)), ((), ())), preferred_element_type=F32
    )


def attention_kernel(scale, group, window, at_ref, length_ref, seg_ref, q_ref, up_ref, *refs):
    pairs = [r[...] for r in refs[: BACK + 1]]
    gq_ref, own_ref = refs[BACK + 1], refs[BACK + 2]
    out_refs = refs[BACK + 3 : 2 * BACK + 3]
    ds_ref, p_ref, bias_ref = refs[2 * BACK + 3 :]
    hd = pairs[0].shape[1] // 2
    rows = q_ref.shape[0]
    keys = jnp.concatenate([p[:, :hd] for p in pairs], axis=0)
    values = jnp.concatenate([p[:, hd:] for p in pairs], axis=0)
    first = pl.multiple_of(at_ref[1], rows)
    place = first + lax.broadcasted_iota(jnp.int32, (1, rows), 1)
    own_seg = seg_ref[:, pl.ds(first, rows)]
    seg_row = seg_ref[...]
    lower = [jnp.sum((seg_row < n).astype(jnp.int32), axis=1, keepdims=True) for n in (1, 2)]
    start = jnp.where(own_seg == 0, 0, jnp.where(own_seg == 1, lower[0], lower[1]))
    low = jnp.maximum(start, place - (window - 1))
    high = jnp.minimum(place, length_ref[0])
    live = (place < length_ref[0]).astype(F32)
    live = jnp.concatenate([live] * 2, axis=1)
    size = pairs[0].shape[0]
    for k in range(BACK + 1):
        key_place = at_ref[0] - k * size + lax.broadcasted_iota(jnp.int32, (size, rows), 0)
        allowed = ((key_place >= low) & (key_place < high)) | (key_place == place)
        bias_ref[k * size : (k + 1) * size, :] = jnp.where(allowed, 0.0, NEG)
    keys_turned = keys.T
    for h in range(0, group, 2):
        heads = [slice(g * hd, (g + 1) * hd) for g in (h, h + 1)]
        cols = slice(h * rows, (h + 2) * rows)
        q_two = jnp.concatenate([q_ref[:, s] for s in heads], axis=0)
        up_two = jnp.concatenate([up_ref[:, s] for s in heads], axis=0)
        bias = jnp.concatenate([bias_ref[...]] * 2, axis=1)
        scores = contract(keys, q_two, 1, 1) * scale + bias
        top = jnp.max(scores, axis=0, keepdims=True)
        raised = jnp.exp(scores - top)
        probs = raised * (live / jnp.sum(raised, axis=0, keepdims=True))
        dprobs = contract(values, up_two, 1, 1)
        rowdot = jnp.sum(probs * dprobs, axis=0, keepdims=True)
        dscores = (probs * (dprobs - rowdot)).astype(BF16)
        ds_ref[:, cols] = dscores
        p_ref[:, cols] = probs.astype(BF16)
        grad_q = (contract(keys_turned, dscores, 1, 0).T * scale).astype(BF16)
        for n, s in enumerate(heads):
            gq_ref[:, s] = grad_q[n * rows : (n + 1) * rows]
    q_all = jnp.concatenate([q_ref[:, g * hd : (g + 1) * hd] for g in range(group)], axis=0)
    up_all = jnp.concatenate([up_ref[:, g * hd : (g + 1) * hd] for g in range(group)], axis=0)
    grad_k = contract(ds_ref[...], q_all, 1, 0) * scale
    grad_v = contract(p_ref[...], up_all, 1, 0)
    own_ref[:, :hd] = grad_k[:size]
    own_ref[:, hd:] = grad_v[:size]
    for k, ref in enumerate(out_refs, 1):
        ref[:, :hd] = grad_k[k * size : (k + 1) * size].astype(BF16)
        ref[:, hd:] = grad_v[k * size : (k + 1) * size].astype(BF16)


def attention(at, lengths, segments, queries, upstream, pairs, scale, window):
    rows, wide = queries.shape
    size, two = pairs[0].shape
    group = wide // (two // 2)
    total = size * (BACK + 1)

    def kernel(*refs):
        attention_kernel(scale, group, window, *refs)

    return pl.pallas_call(
        kernel,
        out_shape=[jax.ShapeDtypeStruct((rows, wide), BF16)]
        + [jax.ShapeDtypeStruct((size, two), F32)]
        + [jax.ShapeDtypeStruct((size, two), BF16)] * BACK,
        in_specs=[pl.BlockSpec(memory_space=pltpu.SMEM)] * 2
        + [pl.BlockSpec(memory_space=pltpu.VMEM)] * (4 + BACK),
        scratch_shapes=[pltpu.VMEM((total, rows * group), BF16)] * 2
        + [pltpu.VMEM((total, rows), F32)],
        cost_estimate=pl.CostEstimate(
            flops=5 * 2 * total * rows * wide,
            bytes_accessed=4 * total * two,
            transcendentals=total * rows * group,
        ),
        compiler_params=pltpu.CompilerParams(vmem_limit_bytes=32 << 20),
        name="window_attention",
    )(at, lengths, segments, queries, upstream, *pairs)


def weights_kernel(at_ref, *refs):
    inputs, grads, out_ref = refs[:4], refs[4:7], refs[7]
    rows = grads[0].shape[0] // 2
    total = None
    for n, x in enumerate(inputs):
        at = pl.ds(pl.multiple_of(at_ref[n % 2] * rows, rows), rows)
        if n < 2:
            parts = [grads[0][at, :], grads[1][at, :]]
        else:
            parts = [grads[2][0, at, :], grads[2][1, at, :]]
        term = contract(x[...], jnp.concatenate(parts, axis=0), 1, 0)
        total = term if total is None else total + term
    out_ref[...] = total.astype(BF16)


def weight_partials(at, inputs, grads, steps):
    count, deep = inputs[0].shape
    tall = count // steps
    wide = grads[0].shape[1]
    return pl.pallas_call(
        weights_kernel,
        out_shape=jax.ShapeDtypeStruct((count, wide), BF16),
        grid=(steps,),
        in_specs=[pl.BlockSpec(memory_space=pltpu.SMEM)]
        + [pl.BlockSpec((tall, deep), lambda j: (j, 0))] * 4
        + [pl.BlockSpec(grads[0].shape, lambda j: (0, 0))] * 2
        + [pl.BlockSpec(grads[2].shape, lambda j: (0, 0, 0))],
        out_specs=pl.BlockSpec((tall, wide), lambda j: (j, 0)),
        cost_estimate=pl.CostEstimate(
            flops=2 * count * wide * deep * 4,
            bytes_accessed=2 * deep * 4 * (count + wide),
            transcendentals=0,
        ),
        compiler_params=pltpu.CompilerParams(vmem_limit_bytes=16 << 20),
        name="weight_partials",
    )(at, *inputs, *grads)


def y_shift(x, by):
    count = lax.axis_size("y")
    return lax.ppermute(x, "y", [(i, i + by) for i in range(count) if 0 <= i + by < count])


def flipped(x, axis):
    return lax.ppermute(x, axis, [(0, 1), (1, 0)])


def x_swap(x, flip_low, flip_high):
    pairs = [(i, i ^ (2 * flip_low + flip_high)) for i in range(4)]
    return lax.ppermute(x, ("x_lo", "x_hi"), pairs)


STEPS = range(1, BACK + 1)


def step(layer_input, queries, key_rows, value_rows, grad_output, segments, lengths):
    y_count = lax.axis_size("y")
    z_count = lax.axis_size("z")
    dp_count = 4 * z_count
    x_lo = lax.axis_index("x_lo")
    core = lax.axis_index("core")
    y_at = lax.axis_index("y")
    x_hi = lax.axis_index("x_hi")
    rows = layer_input.shape[1]
    width_all = layer_input.shape[2]
    head_size = key_rows.shape[2]
    pair_rows = 2 * rows
    scale = 1.0 / math.sqrt(head_size)

    local_pair = jnp.concatenate([key_rows[0], value_rows[0]], axis=1)
    other_pair = flipped(local_pair, "x_hi")
    both = jnp.concatenate(
        [
            jnp.where(x_hi == 0, local_pair, other_pair),
            jnp.where(x_hi == 0, other_pair, local_pair),
        ],
        axis=0,
    )
    pairs = [both]
    for k in range(1, BACK):
        pairs.append(y_shift(both, k))
    half = BACK // 2
    if y_count == 2 * BACK:
        first = [(i, (i - half) % y_count) for i in range(BACK)]
        second = [((i - half) % y_count, i + BACK) for i in range(BACK)]
        passing = lax.ppermute(both, "y", first)
        pairs.append(lax.ppermute(passing, "y", second))
    else:
        pairs.append(y_shift(both, BACK))

    fine = width_all // (2 * z_count * 2 * y_count * 2)
    count = z_count * y_count * fine
    turned = layer_input[0].T
    columns = turned.reshape(2, z_count, 2, y_count, 2, fine, rows)
    to_core = lax.dynamic_slice(
        columns, (0, 0, 1 - core, 0, 0, 0, 0), (2, z_count, 1, y_count, 2, fine, rows)
    )
    from_core = flipped(to_core.reshape(4 * count, rows), "core")
    core_columns = from_core.reshape(2, z_count, y_count, 2, fine, rows)

    def piece(flip_low, flip_high):
        low_to, high_to = x_lo ^ flip_low, x_hi ^ flip_high
        mine = lax.dynamic_slice(
            columns,
            (low_to, 0, core, 0, high_to, 0, 0),
            (1, z_count, 1, y_count, 1, fine, rows),
        )
        theirs = lax.dynamic_slice(
            core_columns, (low_to, 0, 0, high_to, 0, 0), (1, z_count, y_count, 1, fine, rows)
        )
        return jnp.concatenate([mine.reshape(count, rows), theirs.reshape(count, rows)], axis=1)

    inputs = [piece(0, 0)]
    for flips in ((0, 1), (1, 0), (1, 1)):
        inputs.append(x_swap(piece(*flips), *flips))

    base = y_at * pair_rows
    where = jnp.stack([base, base + x_hi * rows]).astype(jnp.int32)
    grad_q, own, *low = attention(
        where, lengths, segments, queries[0], grad_output[0], pairs, scale, 8 * rows
    )

    total = own
    for k in STEPS:
        came = y_shift(low[k - 1], -k)
        total = total + came.astype(F32)
    came = flipped(total.astype(BF16), "x_hi")
    grad_kv = (total + came.astype(F32)).astype(BF16)
    core_grad = flipped(grad_kv, "core")
    x_grads = flipped(jnp.stack([grad_kv, core_grad]), "x_lo")
    at = jnp.stack([x_hi, 1 - x_hi]).astype(jnp.int32)
    partial_value = weight_partials(at, inputs, [grad_kv, core_grad, x_grads], 4)

    peers = z_count * y_count
    pieces = partial_value.reshape(peers, fine, 2 * head_size)
    moved = lax.all_to_all(pieces, ("z", "y"), split_axis=0, concat_axis=0, tiled=True)
    summed = jnp.sum(moved.astype(F32), axis=0)
    grad_weights = (summed / dp_count).astype(BF16)
    return (grad_q[None], grad_weights)


def solution(mesh):
    devices = mesh.devices
    dp_count, ctx_count = devices.shape
    fine = Mesh(devices.reshape(2, dp_count // 4, 2, ctx_count // 2, 2), NAMES)
    return jax.shard_map(
        step,
        mesh=fine,
        in_specs=(
            P(DP, CTX, None),
            P(DP, CTX, None),
            P(DP, CTX, None),
            P(DP, CTX, None),
            P(DP, CTX, None),
            P(DP, None),
            P(DP),
        ),
        out_specs=(P(DP, CTX, None), P(NAMES, None)),
        check_vma=False,
    )
```

```python
import math

import jax
import jax.numpy as jnp
from jax import lax
from jax.experimental import pallas as pl
from jax.experimental.pallas import tpu as pltpu
from jax.sharding import Mesh, PartitionSpec as P


NAMES = ("x_lo", "z", "core", "y", "x_hi")
DP = NAMES[:3]
CTX = NAMES[3:]
BACK = 4
NEG = -1e30
BF16 = jnp.bfloat16
F32 = jnp.float32


def contract(a, b, dim_a, dim_b):
    return lax.dot_general(
        a, b, (((dim_a,), (dim_b,)), ((), ())), preferred_element_type=F32
    )


def attention_kernel(scale, group, window, at_ref, length_ref, seg_ref, q_ref, up_ref, *refs):
    pairs = [r[...] for r in refs[: BACK + 1]]
    gq_ref, own_ref = refs[BACK + 1], refs[BACK + 2]
    out_refs = refs[BACK + 3 : 2 * BACK + 3]
    ds_ref, p_ref, bias_ref = refs[2 * BACK + 3 :]
    hd = pairs[0].shape[1] // 2
    rows = q_ref.shape[0]
    keys = jnp.concatenate([p[:, :hd] for p in pairs], axis=0)
    values = jnp.concatenate([p[:, hd:] for p in pairs], axis=0)
    first = pl.multiple_of(at_ref[1], rows)
    place = first + lax.broadcasted_iota(jnp.int32, (1, rows), 1)
    own_seg = seg_ref[:, pl.ds(first, rows)]
    seg_row = seg_ref[...]
    lower = [jnp.sum((seg_row < n).astype(jnp.int32), axis=1, keepdims=True) for n in (1, 2)]
    start = jnp.where(own_seg == 0, 0, jnp.where(own_seg == 1, lower[0], lower[1]))
    low = jnp.maximum(start, place - (window - 1))
    high = jnp.minimum(place, length_ref[0])
    live = (place < length_ref[0]).astype(F32)
    live = jnp.concatenate([live] * 2, axis=1)
    size = pairs[0].shape[0]
    for k in range(BACK + 1):
        key_place = at_ref[0] - k * size + lax.broadcasted_iota(jnp.int32, (size, rows), 0)
        allowed = ((key_place >= low) & (key_place < high)) | (key_place == place)
        bias_ref[k * size : (k + 1) * size, :] = jnp.where(allowed, 0.0, NEG)
    keys_turned = keys.T
    for h in range(0, group, 2):
        heads = [slice(g * hd, (g + 1) * hd) for g in (h, h + 1)]
        cols = slice(h * rows, (h + 2) * rows)
        q_two = jnp.concatenate([q_ref[:, s] for s in heads], axis=0)
        up_two = jnp.concatenate([up_ref[:, s] for s in heads], axis=0)
        bias = jnp.concatenate([bias_ref[...]] * 2, axis=1)
        scores = contract(keys, q_two, 1, 1) * scale + bias
        top = jnp.max(scores, axis=0, keepdims=True)
        raised = jnp.exp(scores - top)
        probs = raised * (live / jnp.sum(raised, axis=0, keepdims=True))
        dprobs = contract(values, up_two, 1, 1)
        rowdot = jnp.sum(probs * dprobs, axis=0, keepdims=True)
        dscores = (probs * (dprobs - rowdot)).astype(BF16)
        ds_ref[:, cols] = dscores
        p_ref[:, cols] = probs.astype(BF16)
        grad_q = (contract(keys_turned, dscores, 1, 0).T * scale).astype(BF16)
        for n, s in enumerate(heads):
            gq_ref[:, s] = grad_q[n * rows : (n + 1) * rows]
    q_all = jnp.concatenate([q_ref[:, g * hd : (g + 1) * hd] for g in range(group)], axis=0)
    up_all = jnp.concatenate([up_ref[:, g * hd : (g + 1) * hd] for g in range(group)], axis=0)
    grad_k = contract(ds_ref[...], q_all, 1, 0) * scale
    grad_v = contract(p_ref[...], up_all, 1, 0)
    own_ref[:, :hd] = grad_k[:size]
    own_ref[:, hd:] = grad_v[:size]
    for k, ref in enumerate(out_refs, 1):
        ref[:, :hd] = grad_k[k * size : (k + 1) * size].astype(BF16)
        ref[:, hd:] = grad_v[k * size : (k + 1) * size].astype(BF16)


def attention(at, lengths, segments, queries, upstream, pairs, scale, window):
    rows, wide = queries.shape
    size, two = pairs[0].shape
    group = wide // (two // 2)
    total = size * (BACK + 1)

    def kernel(*refs):
        attention_kernel(scale, group, window, *refs)

    return pl.pallas_call(
        kernel,
        out_shape=[jax.ShapeDtypeStruct((rows, wide), BF16)]
        + [jax.ShapeDtypeStruct((size, two), F32)]
        + [jax.ShapeDtypeStruct((size, two), BF16)] * BACK,
        in_specs=[pl.BlockSpec(memory_space=pltpu.SMEM)] * 2
        + [pl.BlockSpec(memory_space=pltpu.VMEM)] * (4 + BACK),
        scratch_shapes=[pltpu.VMEM((total, rows * group), BF16)] * 2
        + [pltpu.VMEM((total, rows), F32)],
        cost_estimate=pl.CostEstimate(
            flops=5 * 2 * total * rows * wide,
            bytes_accessed=4 * total * two,
            transcendentals=total * rows * group,
        ),
        compiler_params=pltpu.CompilerParams(vmem_limit_bytes=32 << 20),
        name="window_attention",
    )(at, lengths, segments, queries, upstream, *pairs)


def weights_kernel(at_ref, *refs):
    inputs, grads, out_ref = refs[:4], refs[4:8], refs[8]
    rows = grads[0].shape[0] // 2
    total = None
    for n, x in enumerate(inputs):
        at = pl.ds(pl.multiple_of(at_ref[n % 2] * rows, rows), rows)
        parts = [g[at, :] for g in grads[n // 2 * 2 :][:2]]
        term = contract(x[...], jnp.concatenate(parts, axis=0), 1, 0)
        total = term if total is None else total + term
    out_ref[...] = total.astype(BF16)


def weight_partials(at, inputs, grads, steps):
    count, deep = inputs[0].shape
    tall = count // steps
    wide = grads[0].shape[1]
    return pl.pallas_call(
        weights_kernel,
        out_shape=jax.ShapeDtypeStruct((count, wide), BF16),
        grid=(steps,),
        in_specs=[pl.BlockSpec(memory_space=pltpu.SMEM)]
        + [pl.BlockSpec((tall, deep), lambda j: (j, 0))] * 4
        + [pl.BlockSpec(grads[0].shape, lambda j: (0, 0))] * 4,
        out_specs=pl.BlockSpec((tall, wide), lambda j: (j, 0)),
        cost_estimate=pl.CostEstimate(
            flops=2 * count * wide * deep * 4,
            bytes_accessed=2 * deep * 4 * (count + wide),
            transcendentals=0,
        ),
        compiler_params=pltpu.CompilerParams(vmem_limit_bytes=16 << 20),
        name="weight_partials",
    )(at, *inputs, *grads)


def y_shift(x, by):
    count = lax.axis_size("y")
    return lax.ppermute(x, "y", [(i, i + by) for i in range(count) if 0 <= i + by < count])


def flipped(x, axis):
    return lax.ppermute(x, axis, [(0, 1), (1, 0)])


def x_swap(x, flip_low, flip_high):
    pairs = [(i, i ^ (2 * flip_low + flip_high)) for i in range(4)]
    return lax.ppermute(x, ("x_lo", "x_hi"), pairs)


STEPS = range(1, BACK + 1)


def step(layer_input, queries, key_rows, value_rows, grad_output, segments, lengths):
    y_count = lax.axis_size("y")
    z_count = lax.axis_size("z")
    dp_count = 4 * z_count
    x_lo = lax.axis_index("x_lo")
    core = lax.axis_index("core")
    y_at = lax.axis_index("y")
    x_hi = lax.axis_index("x_hi")
    rows = layer_input.shape[1]
    width_all = layer_input.shape[2]
    head_size = key_rows.shape[2]
    pair_rows = 2 * rows
    scale = 1.0 / math.sqrt(head_size)

    local_pair = jnp.concatenate([key_rows[0], value_rows[0]], axis=1)
    other_pair = flipped(local_pair, "x_hi")
    both = jnp.concatenate(
        [
            jnp.where(x_hi == 0, local_pair, other_pair),
            jnp.where(x_hi == 0, other_pair, local_pair),
        ],
        axis=0,
    )
    pairs = [both]
    for k in range(1, BACK):
        pairs.append(y_shift(both, k))
    half = BACK // 2
    if y_count == 2 * BACK:
        first = [(i, (i - half) % y_count) for i in range(BACK)]
        second = [((i - half) % y_count, i + BACK) for i in range(BACK)]
        passing = lax.ppermute(both, "y", first)
        pairs.append(lax.ppermute(passing, "y", second))
    else:
        pairs.append(y_shift(both, BACK))

    fine = width_all // (2 * z_count * 2 * y_count * 2)
    count = z_count * y_count * fine
    turned = layer_input[0].T
    columns = turned.reshape(2, z_count, 2, y_count, 2, fine, rows)
    to_core = lax.dynamic_slice(
        columns, (0, 0, 1 - core, 0, 0, 0, 0), (2, z_count, 1, y_count, 2, fine, rows)
    )
    from_core = flipped(to_core.reshape(4 * count, rows), "core")
    core_columns = from_core.reshape(2, z_count, y_count, 2, fine, rows)

    def piece(flip_low, flip_high):
        low_to, high_to = x_lo ^ flip_low, x_hi ^ flip_high
        mine = lax.dynamic_slice(
            columns,
            (low_to, 0, core, 0, high_to, 0, 0),
            (1, z_count, 1, y_count, 1, fine, rows),
        )
        theirs = lax.dynamic_slice(
            core_columns, (low_to, 0, 0, high_to, 0, 0), (1, z_count, y_count, 1, fine, rows)
        )
        return jnp.concatenate([mine.reshape(count, rows), theirs.reshape(count, rows)], axis=1)

    inputs = [piece(0, 0)]
    for flips in ((0, 1), (1, 0), (1, 1)):
        inputs.append(x_swap(piece(*flips), *flips))

    base = y_at * pair_rows
    where = jnp.stack([base, base + x_hi * rows]).astype(jnp.int32)
    grad_q, own, *low = attention(
        where, lengths, segments, queries[0], grad_output[0], pairs, scale, 8 * rows
    )

    total = own
    for k in STEPS:
        came = y_shift(low[k - 1], -k)
        total = total + came.astype(F32)
    came = flipped(total.astype(BF16), "x_hi")
    grad_kv = (total + came.astype(F32)).astype(BF16)
    grads = [grad_kv]
    for axes, flip in (("core", 1), ("x_lo", 1), (("x_lo", "core"), 3)):
        grads.append(lax.ppermute(grad_kv, axes, [(i, i ^ flip) for i in range(flip + 1)]))
    at = jnp.stack([x_hi, 1 - x_hi]).astype(jnp.int32)
    partial_value = weight_partials(at, inputs, grads, 4)

    peers = z_count * y_count
    pieces = partial_value.reshape(peers, fine, 2 * head_size)
    moved = lax.all_to_all(pieces, ("z", "y"), split_axis=0, concat_axis=0, tiled=True)
    summed = jnp.sum(moved.astype(F32), axis=0)
    grad_weights = (summed / dp_count).astype(BF16)
    return (grad_q[None], grad_weights)


def solution(mesh):
    devices = mesh.devices
    dp_count, ctx_count = devices.shape
    fine = Mesh(devices.reshape(2, dp_count // 4, 2, ctx_count // 2, 2), NAMES)
    return jax.shard_map(
        step,
        mesh=fine,
        in_specs=(
            P(DP, CTX, None),
            P(DP, CTX, None),
            P(DP, CTX, None),
            P(DP, CTX, None),
            P(DP, CTX, None),
            P(DP, None),
            P(DP),
        ),
        out_specs=(P(DP, CTX, None), P(NAMES, None)),
        check_vma=False,
    )
```
